1024 devices in a mesh: dp: 64 (over y_hi, z), ctx: 16 (over x, y_lo, core).
Axes of the slice: x: 4, y: 8 (y_hi: 4, y_lo: 2; y = y_hi * 2 + y_lo), z: 16, core: 2. Of those that a mesh axis runs over, the one named last changes fastest.
Arguments:
- queries: bfloat16 [64, 2048, 16, 128], P('dp', 'ctx'), may hold values from -6 to 6
- keys: bfloat16 [64, 2048, 16, 128], P('dp', 'ctx'), may hold values from -6 to 6
- values: bfloat16 [64, 2048, 16, 128], P('dp', 'ctx'), may hold values from -6 to 6
- out_grad: bfloat16 [64, 2048, 16, 128], P('dp', 'ctx'), may hold values from -0.59765625 to 0.59765625
- gate_weight: bfloat16 [16, 128], P(None, 'dp'), may hold values from -0.5 to 0.5
- head_bias: bfloat16 [16], replicated, as said below
Outputs:
- query_grad: bfloat16 [64, 2048, 16, 128], P('dp', 'ctx')
- key_grad: bfloat16 [64, 2048, 16, 128], P('dp', 'ctx')
- gate_grad: float32 [16, 128], P(None, 'dp')
The draws below stay inside these ranges and needn't reach their ends.
Inputs may be any that keep to these rules, and one draw needn't show every extreme that they name: `head_bias`: each entry lies between -ln(2048) - 1.5 and -3.5.
All inputs are finite; a program needn't handle non-finite values.
Results may differ from the reference program's by a relative error of at most 0.0038.
The reference program's roundings to bfloat16 on the way count: a program that leaves them out, or rounds other values in their place, can miss the bound.
Values may be sent and summed in bfloat16 or wider, within the bound.
A program may use at most 128 MiB of HBM per device.

```python
import jax
import jax.numpy as jnp
from jax import lax

H = 16
HD = 128
TOK_DEV = 128
LENGTH = 2048
HISTS = 64


def draw_head_bias(key, part):
    first, second, third = jax.random.split(jax.random.fold_in(key, 17), 3)
    share = 0.5
    quick = jax.random.uniform(first, (H,)) < share
    slow = -jnp.log(jnp.float32(LENGTH)) + jax.random.uniform(second, (H,), jnp.float32, -1.5, 0.0)
    fast = jax.random.uniform(third, (H,), jnp.float32, -4.8, -3.6)
    return jnp.where(quick, fast, slow).astype(jnp.bfloat16)


def level_of(rng, shape, cuts, low, largest):
    def one(axis_at, blocks):
        steps = jax.random.uniform(jax.random.fold_in(jax.random.fold_in(rng, 6), axis_at), (blocks,), jnp.float32, low / len(cuts), largest / len(cuts))
        return jnp.repeat(jnp.exp(steps), shape[axis_at] // blocks).reshape((-1,) + (1,) * (len(shape) - axis_at - 1))

    factor_of = one(*cuts[0])
    for cut in cuts[1:]:
        factor_of = factor_of * one(*cut)
    return factor_of


def centred(stream_key, extent, scale, limit, cuts=(), held_as=jnp.bfloat16):
    drawn = scale * jax.random.normal(stream_key, extent, jnp.float32)
    if cuts:
        drawn = drawn * level_of(stream_key, extent, cuts, -0.22, 0.18)
    return jnp.clip(drawn, -limit, limit).astype(held_as)


def setup_inputs(seed: int = 0) -> dict:
    key_list = jax.random.split(jax.random.key(seed), 7)
    queries = centred(key_list[0], (HISTS, LENGTH, H, HD), 1.0, 6.0, ((0, 64), (1, 16)))
    keys = centred(key_list[1], (HISTS, LENGTH, H, HD), 1.0, 6.0, ((0, 64), (1, 16)))
    values = centred(key_list[2], (HISTS, LENGTH, H, HD), 1.0, 6.0, ((0, 64), (1, 16)))
    out_grad = centred(key_list[3], (HISTS, LENGTH, H, HD), 0.088, 0.59765625, ((0, 64), (1, 16)))
    gate_weight = centred(key_list[4], (H, HD), HD ** -0.5, 0.5, ((1, 64),))
    head_bias = draw_head_bias(jax.random.fold_in(key_list[6], 71), 0)
    return dict(queries=queries, keys=keys, values=values, out_grad=out_grad, gate_weight=gate_weight, head_bias=head_bias)


def gate_logit(keys_block, gate_rows, bias_rows):
    return jnp.sum(keys_block.astype(jnp.float32) * gate_rows.astype(jnp.float32)[None], -1) + bias_rows.astype(jnp.float32)[None]


def key_state(keys_block, values_block, cumul):
    tail = jnp.exp(cumul[-1][None] - cumul)[:, :, None]
    scaled = (keys_block.astype(jnp.float32) * tail).astype(jnp.bfloat16)
    return jnp.exp(cumul[-1]), jnp.einsum('chd,che->hde', scaled, values_block, preferred_element_type=jnp.float32)


def query_state(queries_block, grads_block, cumul):
    head = jnp.exp(cumul)[:, :, None]
    scaled = (queries_block.astype(jnp.float32) * head).astype(jnp.bfloat16)
    return jnp.exp(cumul[-1]), jnp.einsum('chd,che->hde', scaled, grads_block, preferred_element_type=jnp.float32)


def block_grads(queries_block, keys_block, values_block, grads_block, cumul, incoming, outgoing, scale):
    count = queries_block.shape[0]
    rows = lax.broadcasted_iota(jnp.int32, (count, count), 0)
    cols = lax.broadcasted_iota(jnp.int32, (count, count), 1)
    causal = rows >= cols
    trans = cumul.T
    gap = trans[:, :, None] - trans[:, None, :]
    decay = jnp.exp(jnp.where(causal[None], gap, -1e30))
    products = jnp.einsum('the,she->hts', grads_block, values_block, preferred_element_type=jnp.float32)
    wround = (scale * products * decay).astype(jnp.bfloat16)
    head = jnp.exp(cumul)[:, :, None]
    tail = jnp.exp(cumul[-1][None] - cumul)[:, :, None]
    in_round = incoming.astype(jnp.bfloat16)
    out_round = outgoing.astype(jnp.bfloat16)
    qgrad = jnp.einsum('hts,shd->thd', wround, keys_block, preferred_element_type=jnp.float32) + scale * head * jnp.einsum('the,hde->thd', grads_block, in_round, preferred_element_type=jnp.float32)
    kgrad = jnp.einsum('hts,thd->shd', wround, queries_block, preferred_element_type=jnp.float32) + scale * tail * jnp.einsum('she,hde->shd', values_block, out_round, preferred_element_type=jnp.float32)
    dgsum = jnp.sum(queries_block.astype(jnp.float32) * qgrad, -1) - jnp.sum(keys_block.astype(jnp.float32) * kgrad, -1)
    return qgrad, kgrad, dgsum


def finish(qgrad, kgrad, dgsum, after, logit, keys_block, gate_rows):
    total = after[None] + jnp.sum(dgsum, 0)[None] - jnp.cumsum(dgsum, 0) + dgsum
    dlogit = -jax.nn.sigmoid(logit) * total
    rounded = lax.optimization_barrier(kgrad.astype(jnp.bfloat16)).astype(jnp.float32)
    key_out = (rounded + dlogit[:, :, None] * gate_rows.astype(jnp.float32)[None]).astype(jnp.bfloat16)
    weight_term = jnp.sum(dlogit[:, :, None] * keys_block.astype(jnp.float32), 0)
    return qgrad.astype(jnp.bfloat16), key_out, weight_term


def sequence_grads(queries_seq, keys_seq, values_seq, grads_seq, gate_rows, bias_rows, block):
    length, heads, width = queries_seq.shape
    count = length // block
    scale = 1.0 / width
    logit = gate_logit(keys_seq, gate_rows, bias_rows)
    cumul = jnp.cumsum(-jax.nn.softplus(logit).reshape(count, block, heads), axis=1)
    logit_blocks = logit.reshape(count, block, heads)

    def split(array):
        return array.reshape(count, block, heads, width)

    qb, kb, vb, gb = split(queries_seq), split(keys_seq), split(values_seq), split(grads_seq)
    zeros = jnp.zeros((heads, width, width), jnp.float32)

    def forward(state, items):
        kx, vx, cx = items
        factor, update = key_state(kx, vx, cx)
        return factor[:, None, None] * state + update, state

    _, incoming = lax.scan(forward, zeros, (kb, vb, cumul))

    def backward(carry, items):
        outgoing, after, accum = carry
        qx, kx, vx, gx, cx, sx, lx = items
        factor, update = query_state(qx, gx, cx)
        qgrad, kgrad, dgsum = block_grads(qx, kx, vx, gx, cx, sx, outgoing, scale)
        qout, kout, term = finish(qgrad, kgrad, dgsum, after, lx, kx, gate_rows)
        return (factor[:, None, None] * outgoing + update, after + jnp.sum(dgsum, 0), accum + term), (qout, kout)

    start = (zeros, jnp.zeros((heads,), jnp.float32), jnp.zeros((heads, width), jnp.float32))
    (_, _, accum), (qouts, kouts) = lax.scan(backward, start, (qb, kb, vb, gb, cumul, incoming, logit_blocks), reverse=True)
    return qouts.reshape(length, heads, width), kouts.reshape(length, heads, width), accum


def reference(queries, keys, values, out_grad, gate_weight, head_bias):
    def single(items):
        qx, kx, vx, gx = items
        return sequence_grads(qx, kx, vx, gx, gate_weight, head_bias, TOK_DEV)

    query_grad, key_grad, terms = lax.map(single, (queries, keys, values, out_grad))
    return query_grad, key_grad, jnp.sum(terms, 0)
```

```python
import functools

import jax
import jax.numpy as jnp
from jax import lax
from jax.experimental import pallas as pl
from jax.experimental.pallas import tpu as pltpu
from jax.sharding import PartitionSpec as P

F32 = jnp.float32
BF16 = jnp.bfloat16
MESH = pl.DeviceIdType.MESH
K, V, G, Q = 0, 1, 2, 3
ZN = 16


def iota(shape, dim):
    return lax.broadcasted_iota(jnp.int32, shape, dim)


def dot(a, b, dims, precision=None):
    return lax.dot_general(
        a, b, (dims, ((), ())), precision=precision, preferred_element_type=F32
    )


NN = ((1,), (0,))
NT = ((1,), (1,))
TN = ((0,), (0,))
EXACT = lax.Precision.HIGHEST


def log1p(y):
    u = 1.0 + y
    d = u - 1.0
    return jnp.where(d == 0.0, y, jnp.log(u) * (y / jnp.where(d == 0.0, 1.0, d)))


class Exchange:
    def __init__(self, n, me, where, own, slots, ssem, rsem):
        self.n, self.me, self.where = n, me, where
        self.own, self.slots, self.ssem, self.rsem = own, slots, ssem, rsem

    def copy(self, j, slot, target):
        return pltpu.make_async_remote_copy(
            src_ref=self.own,
            dst_ref=self.slots.at[slot],
            send_sem=self.ssem.at[j],
            recv_sem=self.rsem.at[slot],
            device_id=self.where(target),
            device_id_type=MESH,
        )

    def start(self, row):
        self.own[...] = row
        self.slots[self.me] = row

        def go(j, _):
            self.copy(j, self.me, lax.rem(self.me + j, self.n)).start()
            return 0

        lax.fori_loop(1, self.n, go, 0)

    def finish(self):
        def go(j, _):
            s = lax.rem(self.me + j, self.n)
            self.copy(j, s, s).wait()
            return 0

        lax.fori_loop(1, self.n, go, 0)


def kernel(
    k_in, v_in, g_in, q_in, gw_ref, hb_ref,
    qo_out, ko_out, gg_ref,
    raw, raw32, sb, rb, colb, rowb, lastb, kvr, wts, qf, out_s, out_r, packed, lrow, square,
    wy_own, wy_slots, wz_own, wz_slots, dz_own, dz_slots, dy_own, dy_slots, dc_own, dc_slots,
    lsem, osem, in_s, in_rs, back_s, back_rs, own_sem, own_back,
    wy_s, wy_r, wz_s, wz_r, dz_s, dz_r, dy_s, dy_r, dc_s, dc_r,
):
    yn = wy_slots.shape[0]
    heads = sb.shape[1]
    tok = sb.shape[2]
    width = sb.shape[3]
    scale = 1.0 / width
    i = lax.axis_index("dp")
    c = lax.axis_index("ctx")
    yh = i // ZN
    z = lax.rem(i, ZN)

    def at_ctx(t):
        return {"ctx": t}

    def at_z(t):
        return {"dp": yh * ZN + t}

    def at_y(t):
        return {"dp": t * ZN + z}

    loads = [
        pltpu.make_async_copy(src, raw.at[a], lsem.at[a])
        for a, src in enumerate((k_in, v_in, g_in, q_in))
    ]
    for load in loads:
        load.start()

    barrier = pltpu.get_barrier_semaphore()
    for n, me, where in ((ZN, z, at_z), (yn, yh, at_y), (heads, c, at_ctx)):

        def greet(j, _, n=n, me=me, where=where):
            pl.semaphore_signal(
                barrier, inc=1, device_id=where(lax.rem(me + j, n)), device_id_type=MESH
            )
            return 0

        lax.fori_loop(1, n, greet, 0)

    gw = gw_ref[...].astype(F32)
    picked = jnp.sum(jnp.where(iota(gw.shape, 0) == c, gw, 0.0), axis=0, keepdims=True)
    lane = iota((1, width), 1)
    own_row = jnp.where(lane == 2 * i, picked[:, 0:1], 0.0) + jnp.where(
        lane == 2 * i + 1, picked[:, 1:2], 0.0
    )
    hb = hb_ref[...].astype(F32)
    bias = jnp.sum(jnp.where(iota(hb.shape, 1) == c, hb, 0.0), axis=1, keepdims=True)

    def split_heads(a):
        loads[a].wait()
        raw32[...] = raw[a].astype(F32)
        for h in range(heads):
            sb[a, h] = raw32[pl.ds(h, tok, stride=heads), :].astype(BF16)

    def bulk(a, j, slot, target):
        return pltpu.make_async_remote_copy(
            src_ref=sb.at[a, target],
            dst_ref=rb.at[a, slot],
            send_sem=in_s.at[a, j],
            recv_sem=in_rs.at[a, slot],
            device_id=at_ctx(target),
            device_id_type=MESH,
        )

    def own_in(a):
        return pltpu.make_async_copy(sb.at[a, c], rb.at[a, c], own_sem.at[a])

    def send_heads(a):
        def go(j, _):
            bulk(a, j, c, lax.rem(c + j, heads)).start()
            return 0

        lax.fori_loop(1, heads, go, 0)
        own_in(a).start()

    def wait_heads(a):
        def go(j, _):
            s = lax.rem(c + j, heads)
            bulk(a, j, s, s).wait_recv()
            return 0

        lax.fori_loop(1, heads, go, 0)
        own_in(a).wait()

    wy = Exchange(yn, yh, at_y, wy_own, wy_slots, wy_s, wy_r)
    wz = Exchange(ZN, z, at_z, wz_own, wz_slots, wz_s, wz_r)
    split_heads(K)
    pl.semaphore_wait(barrier, (ZN - 1) + (yn - 1) + (heads - 1))
    wy.start(own_row)
    send_heads(K)
    split_heads(V)
    send_heads(V)
    wy.finish()
    wz.start(jnp.sum(wy_slots[...], axis=0))
    split_heads(G)
    send_heads(G)
    split_heads(Q)
    send_heads(Q)
    wz.finish()
    gate = jnp.sum(wz_slots[...], axis=0)

    wait_heads(K)
    gate8 = jnp.broadcast_to(gate, (8, width)).astype(BF16)
    for b in range(heads):
        lrow[b : b + 1, :] = dot(gate8, rb[K, b], NT)[0:1]
    logit = lrow[...] + bias
    decay = -(jnp.maximum(logit, 0.0) + log1p(jnp.exp(-jnp.abs(logit))))
    upper = (iota((tok, tok), 0) <= iota((tok, tok), 1)).astype(F32)
    cumul = dot(decay, upper, NN, EXACT)
    square[...] = jnp.zeros_like(square)
    square[0:heads, :] = cumul
    cumul_t = square[...].T
    square[0:heads, :] = logit
    logit_t = square[...].T
    for b in range(heads):
        colb[b] = jnp.broadcast_to(cumul_t[:, b : b + 1], (tok, width))
        rowb[b] = cumul[b : b + 1, :]
        lastb[b] = jnp.broadcast_to(cumul[b : b + 1, tok - 1 : tok], (1, width))

    wait_heads(V)

    def forward(b, state):
        kvr[b] = state.astype(BF16)
        tail = jnp.exp(lastb[b] - colb[b])
        scaled = (rb[K, b].astype(F32) * tail).astype(BF16)
        return jnp.exp(lastb[b]) * state + dot(rb[V, b], scaled, TN)

    lax.fori_loop(0, heads, forward, jnp.zeros((width, width), F32), unroll=4)

    wait_heads(G)

    def back(which, j, slot, target):
        return pltpu.make_async_remote_copy(
            src_ref=out_s.at[which, target],
            dst_ref=out_r.at[which, slot],
            send_sem=back_s.at[which, j],
            recv_sem=back_rs.at[which, slot],
            device_id=at_ctx(target),
            device_id_type=MESH,
        )

    def own_out(which):
        return pltpu.make_async_copy(out_s.at[which, c], out_r.at[which, c], own_back.at[which])

    causal = iota((tok, tok), 0) >= iota((tok, tok), 1)

    def query_block(b):
        kx, vx, gx = rb[K, b], rb[V, b], rb[G, b]
        gap = colb[b] - rowb[b]
        fade = jnp.exp(jnp.where(causal, gap, -1e30))
        weight = (scale * dot(gx, vx, NT) * fade).astype(BF16)
        wts[b] = weight
        full = dot(weight, kx, NN) + scale * jnp.exp(colb[b]) * dot(gx, kvr[b], NN)
        qf[b] = full
        out_s[0, b] = full.astype(BF16)

    query_block(c)
    own_out(0).start()

    def query_step(j, _):
        b = lax.rem(c + j, heads)
        query_block(b)
        back(0, j, c, b).start()
        return 0

    lax.fori_loop(1, heads, query_step, 0, unroll=3)

    wait_heads(Q)

    def backward(j, carry):
        b = heads - 1 - j
        state, dg_t = carry
        kx, vx, gx, qx = rb[K, b], rb[V, b], rb[G, b], rb[Q, b]
        col, last = colb[b], lastb[b]
        tail = jnp.exp(last - col)
        kattn = dot(wts[b], qx, TN) + scale * tail * dot(vx, state.astype(BF16), NN)
        out_s[1, b] = kattn.astype(BF16)
        qx32 = qx.astype(F32)
        diff = jnp.sum(qx32 * qf[b] - kx.astype(F32) * kattn, axis=1, keepdims=True)
        dg_t = jnp.where(iota(dg_t.shape, 1) == b, diff, dg_t)
        scaled = (qx32 * jnp.exp(col)).astype(BF16)
        return jnp.exp(last) * state + dot(gx, scaled, TN), dg_t

    zeros = jnp.zeros((width, width), F32)
    _, dg_t = lax.fori_loop(0, heads, backward, (zeros, zeros), unroll=4)

    later = (iota((tok, tok), 0) <= iota((tok, tok), 1)).astype(F32)
    within = dot(later, dg_t, NN, EXACT)
    after_mat = (iota((width, width), 0) > iota((width, width), 1)).astype(F32)
    after = dot(jnp.broadcast_to(within[0:1, :], (8, width)), after_mat, NN, EXACT)
    dlogit = -(within + after[0:1, :]) / (1.0 + jnp.exp(-logit_t))

    total = zeros
    for b in range(heads):
        dcol = jnp.broadcast_to(dlogit[:, b : b + 1], (tok, width))
        total = total + dcol * rb[K, b].astype(F32)
        out_s[1, b] = (out_s[1, b].astype(F32) + dcol * gate).astype(BF16)

    dz = Exchange(ZN, z, at_z, dz_own, dz_slots, dz_s, dz_r)
    dy = Exchange(yn, yh, at_y, dy_own, dy_slots, dy_s, dy_r)
    dc = Exchange(heads, c, at_ctx, dc_own, dc_slots, dc_s, dc_r)
    dz.start(jnp.sum(total, axis=0, keepdims=True))

    def send_key(j, _):
        back(1, j, c, lax.rem(c + j, heads)).start()
        return 0

    lax.fori_loop(1, heads, send_key, 0)
    own_out(1).start()

    outs = (qo_out, ko_out)

    def join_heads(which):
        def go(j, _):
            s = lax.rem(c + j, heads)
            back(which, j, s, s).wait_recv()
            return 0

        lax.fori_loop(1, heads, go, 0)
        own_out(which).wait()
        for h in range(heads):
            raw32[pl.ds(h, tok, stride=heads), :] = out_r[which, h].astype(F32)
        packed[which] = raw32[...].astype(BF16)
        pltpu.make_async_copy(packed.at[which], outs[which], osem.at[which]).start()

    join_heads(0)
    dz.finish()
    dy.start(jnp.sum(dz_slots[...], axis=0))
    dy.finish()
    dc.start(jnp.sum(dy_slots[...], axis=0))
    join_heads(1)
    dc.finish()
    rows = dc_slots[...].reshape(heads, width)
    at = iota((heads, width), 1)
    left = jnp.sum(jnp.where(at == 2 * i, rows, 0.0), axis=1, keepdims=True)
    right = jnp.sum(jnp.where(at == 2 * i + 1, rows, 0.0), axis=1, keepdims=True)
    gg_ref[...] = jnp.where(iota((heads, 2), 1) == 0, left, right)

    def drain(j, _):
        t = lax.rem(c + j, heads)
        for a in range(4):
            bulk(a, j, c, t).wait_send()
        for which in range(2):
            back(which, j, c, t).wait_send()
        return 0

    lax.fori_loop(1, heads, drain, 0)
    for which in range(2):
        pltpu.make_async_copy(packed.at[which], outs[which], osem.at[which]).wait()


def per_device(queries, keys, values, out_grad, gate_weight, head_bias):
    _, tok, heads, width = queries.shape
    yn = lax.axis_size("dp") // ZN
    rows = tok * heads
    flat = [x.reshape(rows, width) for x in (keys, values, out_grad, queries)]
    vm = pltpu.VMEM
    dma = pltpu.SemaphoreType.DMA

    def slots(n):
        return [vm((1, width), F32), vm((n, 1, width), F32)]

    anywhere = pl.BlockSpec(memory_space=pl.ANY)
    inside = pl.BlockSpec(memory_space=pltpu.VMEM)
    qo, ko, gg = pl.pallas_call(
        kernel,
        name="history_grads",
        out_shape=(
            jax.ShapeDtypeStruct((rows, width), BF16),
            jax.ShapeDtypeStruct((rows, width), BF16),
            jax.ShapeDtypeStruct((heads, 2), F32),
        ),
        in_specs=[anywhere] * 4 + [inside] * 2,
        out_specs=(anywhere, anywhere, inside),
        scratch_shapes=[
            vm((4, rows, width), BF16),
            vm((rows, width), F32),
            vm((4, heads, tok, width), BF16),
            vm((4, heads, tok, width), BF16),
            vm((heads, tok, width), F32),
            vm((heads, 1, width), F32),
            vm((heads, 1, width), F32),
            vm((heads, width, width), BF16),
            vm((heads, tok, tok), BF16),
            vm((heads, tok, width), F32),
            vm((2, heads, tok, width), BF16),
            vm((2, heads, tok, width), BF16),
            vm((2, rows, width), BF16),
            vm((heads, width), F32),
            vm((width, width), F32),
            *slots(yn), *slots(ZN), *slots(ZN), *slots(yn), *slots(heads),
            dma((4,)), dma((2,)),
            dma((4, heads)), dma((4, heads)),
            dma((2, heads)), dma((2, heads)),
            dma((4,)), dma((2,)),
            dma((yn,)), dma((yn,)), dma((ZN,)), dma((ZN,)),
            dma((ZN,)), dma((ZN,)), dma((yn,)), dma((yn,)), dma((heads,)), dma((heads,)),
        ],
        compiler_params=pltpu.CompilerParams(
            collective_id=0, has_side_effects=True, vmem_limit_bytes=48 * 1024 * 1024
        ),
    )(*flat, gate_weight, head_bias.reshape(1, heads))
    shape = (1, tok, heads, width)
    return qo.reshape(shape), ko.reshape(shape), gg


def solution(mesh):
    return jax.shard_map(
        per_device,
        mesh=mesh,
        in_specs=(
            P("dp", "ctx", None, None),
            P("dp", "ctx", None, None),
            P("dp", "ctx", None, None),
            P("dp", "ctx", None, None),
            P(None, "dp"),
            P(),
        ),
        out_specs=(P("dp", "ctx", None, None), P("dp", "ctx", None, None), P(None, "dp")),
        check_vma=False,
    )
```

```python
import functools

import jax
import jax.numpy as jnp
from jax import lax
from jax.experimental import pallas as pl
from jax.experimental.pallas import tpu as pltpu
from jax.sharding import PartitionSpec as P

F32 = jnp.float32
BF16 = jnp.bfloat16
MESH = pl.DeviceIdType.MESH
K, V, G, Q = 0, 1, 2, 3
ZN = 16
REACH = ZN // 4


def iota(shape, dim):
    return lax.broadcasted_iota(jnp.int32, shape, dim)


def dot(a, b, dims, precision=None):
    return lax.dot_general(
        a, b, (dims, ((), ())), precision=precision, preferred_element_type=F32
    )


NN = ((1,), (0,))
NT = ((1,), (1,))
TN = ((0,), (0,))
EXACT = lax.Precision.HIGHEST


def log1p(y):
    u = 1.0 + y
    d = u - 1.0
    return jnp.where(d == 0.0, y, jnp.log(u) * (y / jnp.where(d == 0.0, 1.0, d)))


class Along:
    def __init__(self, me, where, own, slots, ssem, rsem):
        self.me, self.where = me, where
        self.own, self.slots, self.ssem, self.rsem = own, slots, ssem, rsem

    def copy(self, src, j, step):
        return pltpu.make_async_remote_copy(
            src_ref=self.own.at[src],
            dst_ref=self.slots.at[j],
            send_sem=self.ssem.at[j],
            recv_sem=self.rsem.at[j],
            device_id=self.where(lax.rem(self.me + step + ZN, ZN)),
            device_id_type=MESH,
        )

    def near(self, j):
        return self.copy(0, j, jnp.where(j < REACH, j + 1, REACH - 1 - j))

    def start(self, row):
        self.own[0] = row

        def go(j, _):
            self.near(j).start()
            return 0

        lax.fori_loop(0, 2 * REACH, go, 0)

    def turn(self):
        def go(j, _):
            self.near(j).wait()
            return 0

        lax.fori_loop(0, 2 * REACH, go, 0)
        below = jnp.sum(self.slots[0:REACH], axis=0)
        above = jnp.sum(self.slots[REACH : 2 * REACH - 1], axis=0)
        self.own[1] = below
        self.own[2] = above
        self.far = [self.copy(1, 2 * REACH, REACH), self.copy(2, 2 * REACH + 1, -REACH)]
        for far in self.far:
            far.start()

    def finish(self):
        for far in self.far:
            far.wait()
        return self.own[0] + jnp.sum(self.slots[...], axis=0)


class Exchange:
    def __init__(self, n, me, where, own, slots, ssem, rsem):
        self.n, self.me, self.where = n, me, where
        self.own, self.slots, self.ssem, self.rsem = own, slots, ssem, rsem

    def copy(self, j, slot, target):
        return pltpu.make_async_remote_copy(
            src_ref=self.own,
            dst_ref=self.slots.at[slot],
            send_sem=self.ssem.at[j],
            recv_sem=self.rsem.at[slot],
            device_id=self.where(target),
            device_id_type=MESH,
        )

    def start(self, row):
        self.own[...] = row
        self.slots[self.me] = row

        def go(j, _):
            self.copy(j, self.me, lax.rem(self.me + j, self.n)).start()
            return 0

        lax.fori_loop(1, self.n, go, 0)

    def finish(self):
        def go(j, _):
            s = lax.rem(self.me + j, self.n)
            self.copy(j, s, s).wait()
            return 0

        lax.fori_loop(1, self.n, go, 0)


def kernel(
    k_in, v_in, g_in, q_in, gw_in, hb_in,
    qo_out, ko_out, gg_ref,
    gw_v, hb_v, raw, raw32, sb, rb, colb, rowb, lastb, kvr, wts, qf, qgt, out_s, out_r, packed, lrow, square,
    wy_own, wy_slots, wz_own, wz_slots, dz_own, dz_slots, dy_own, dy_slots, dc_own, dc_slots,
    ssem, lsem, osem, in_s, in_rs, back_s, back_rs, own_sem, own_back,
    wy_s, wy_r, wz_s, wz_r, dz_s, dz_r, dy_s, dy_r, dc_s, dc_r,
):
    yn = wy_slots.shape[0]
    heads = sb.shape[1]
    tok = sb.shape[2]
    width = sb.shape[3]
    scale = 1.0 / width
    i = lax.axis_index("dp")
    c = lax.axis_index("ctx")
    yh = i // ZN
    z = lax.rem(i, ZN)

    def at_ctx(t):
        return {"ctx": t}

    def at_z(t):
        return {"dp": yh * ZN + t}

    def at_y(t):
        return {"dp": t * ZN + z}

    loads = [
        pltpu.make_async_copy(src, raw.at[a], lsem.at[a])
        for a, src in enumerate((k_in, v_in, g_in, q_in))
    ]
    small = [
        pltpu.make_async_copy(src, dst, ssem.at[a])
        for a, (src, dst) in enumerate(((gw_in, gw_v), (hb_in, hb_v)))
    ]
    for load in small + loads:
        load.start()

    barrier = pltpu.get_barrier_semaphore()

    def greet_z(j, _):
        step = jnp.where(j < REACH, j + 1, REACH - 1 - j)
        pl.semaphore_signal(
            barrier, inc=1, device_id=at_z(lax.rem(z + step + ZN, ZN)), device_id_type=MESH
        )
        return 0

    lax.fori_loop(0, 2 * REACH, greet_z, 0)
    for n, me, where in ((yn, yh, at_y), (heads, c, at_ctx)):

        def greet(j, _, n=n, me=me, where=where):
            pl.semaphore_signal(
                barrier, inc=1, device_id=where(lax.rem(me + j, n)), device_id_type=MESH
            )
            return 0

        lax.fori_loop(1, n, greet, 0)

    for load in small:
        load.wait()
    gw = gw_v[...].astype(F32)
    picked = jnp.sum(jnp.where(iota(gw.shape, 1) == c, gw, 0.0), axis=1, keepdims=True)
    lane = iota((1, width), 1)
    own_row = jnp.where(lane == 2 * i, picked[0:1], 0.0) + jnp.where(
        lane == 2 * i + 1, picked[1:2], 0.0
    )
    hb = hb_v[...].astype(F32)
    bias = jnp.sum(jnp.where(iota(hb.shape, 1) == c, hb, 0.0), axis=1, keepdims=True)

    def split_heads(a):
        loads[a].wait()
        raw32[...] = raw[a].astype(F32)
        for h in range(heads):
            sb[a, h] = raw32[pl.ds(h, tok, stride=heads), :].astype(BF16)

    def bulk(a, j, slot, target):
        return pltpu.make_async_remote_copy(
            src_ref=sb.at[a, target],
            dst_ref=rb.at[a, slot],
            send_sem=in_s.at[a, j],
            recv_sem=in_rs.at[a, slot],
            device_id=at_ctx(target),
            device_id_type=MESH,
        )

    def own_in(a):
        return pltpu.make_async_copy(sb.at[a, c], rb.at[a, c], own_sem.at[a])

    def send_heads(a):
        def go(j, _):
            bulk(a, j, c, lax.rem(c + j, heads)).start()
            return 0

        lax.fori_loop(1, heads, go, 0)
        own_in(a).start()

    def wait_heads(a):
        def go(j, _):
            s = lax.rem(c + j, heads)
            bulk(a, j, s, s).wait_recv()
            return 0

        lax.fori_loop(1, heads, go, 0)
        own_in(a).wait()

    wy = Exchange(yn, yh, at_y, wy_own, wy_slots, wy_s, wy_r)
    wz = Along(z, at_z, wz_own, wz_slots, wz_s, wz_r)
    split_heads(K)
    pl.semaphore_wait(barrier, 2 * REACH + (yn - 1) + (heads - 1))
    wy.start(own_row)
    send_heads(K)
    split_heads(V)
    send_heads(V)
    wy.finish()
    wz.start(jnp.sum(wy_slots[...], axis=0))
    split_heads(G)
    send_heads(G)
    split_heads(Q)
    send_heads(Q)
    wz.turn()
    gate = wz.finish()

    wait_heads(K)
    gate8 = jnp.broadcast_to(gate, (8, width)).astype(BF16)
    for b in range(heads):
        lrow[b : b + 1, :] = dot(gate8, rb[K, b], NT)[0:1]
    logit = lrow[...] + bias
    decay = -(jnp.maximum(logit, 0.0) + log1p(jnp.exp(-jnp.abs(logit))))
    upper = (iota((tok, tok), 0) <= iota((tok, tok), 1)).astype(F32)
    cumul = dot(decay, upper, NN, EXACT)
    square[...] = jnp.zeros_like(square)
    square[0:heads, :] = cumul
    cumul_t = square[...].T
    square[0:heads, :] = logit
    logit_t = square[...].T
    for b in range(heads):
        colb[b] = jnp.broadcast_to(cumul_t[:, b : b + 1], (tok, width))
        rowb[b] = cumul[b : b + 1, :]
        lastb[b] = jnp.broadcast_to(cumul[b : b + 1, tok - 1 : tok], (1, width))

    wait_heads(V)

    def forward(b, state):
        kvr[b] = state.astype(BF16)
        tail = jnp.exp(lastb[b] - colb[b])
        scaled = (rb[K, b].astype(F32) * tail).astype(BF16)
        return jnp.exp(lastb[b]) * state + dot(rb[V, b], scaled, TN)

    lax.fori_loop(0, heads, forward, jnp.zeros((width, width), F32), unroll=4)

    wait_heads(G)

    def back(which, j, slot, target):
        return pltpu.make_async_remote_copy(
            src_ref=out_s.at[which, target],
            dst_ref=out_r.at[which, slot],
            send_sem=back_s.at[which, j],
            recv_sem=back_rs.at[which, slot],
            device_id=at_ctx(target),
            device_id_type=MESH,
        )

    def own_out(which):
        return pltpu.make_async_copy(out_s.at[which, c], out_r.at[which, c], own_back.at[which])

    causal = iota((tok, tok), 0) >= iota((tok, tok), 1)

    def query_block(b):
        kx, vx, gx = rb[K, b], rb[V, b], rb[G, b]
        gap = colb[b] - rowb[b]
        fade = jnp.exp(jnp.where(causal, gap, -1e30))
        weight = (scale * dot(gx, vx, NT) * fade).astype(BF16)
        wts[b] = weight
        full = dot(weight, kx, NN) + scale * jnp.exp(colb[b]) * dot(gx, kvr[b], NN)
        qf[b] = full
        out_s[0, b] = full.astype(BF16)

    query_block(c)
    own_out(0).start()

    def query_step(j, _):
        b = lax.rem(c + j, heads)
        query_block(b)
        back(0, j, c, b).start()
        return 0

    lax.fori_loop(1, heads, query_step, 0, unroll=3)

    zeros = jnp.zeros((width, width), F32)

    def arrival(b, dg_t):
        gx, qx = rb[G, b], rb[Q, b]
        qx32 = qx.astype(F32)
        diff = jnp.sum(qx32 * qf[b], axis=1, keepdims=True)
        qf[b] = dot(wts[b], qx, TN)
        qgt[b] = dot(gx, (qx32 * jnp.exp(colb[b])).astype(BF16), TN)
        return jnp.where(iota(dg_t.shape, 1) == b, diff, dg_t)

    own_in(Q).wait()

    def arrival_step(j, dg_t):
        s = lax.rem(c + heads - j, heads)
        bulk(Q, j, s, s).wait_recv()
        return arrival(s, dg_t)

    dg_t = lax.fori_loop(1, heads, arrival_step, arrival(c, zeros), unroll=3)

    def backward(j, carry):
        b = heads - 1 - j
        state, dg_t = carry
        last = lastb[b]
        tail = jnp.exp(last - colb[b])
        kattn = qf[b] + scale * tail * dot(rb[V, b], state.astype(BF16), NN)
        out_s[1, b] = kattn.astype(BF16)
        diff = jnp.sum(rb[K, b].astype(F32) * kattn, axis=1, keepdims=True)
        dg_t = dg_t - jnp.where(iota(dg_t.shape, 1) == b, diff, 0.0)
        return jnp.exp(last) * state + qgt[b], dg_t

    _, dg_t = lax.fori_loop(0, heads, backward, (zeros, dg_t), unroll=4)

    later = (iota((tok, tok), 0) <= iota((tok, tok), 1)).astype(F32)
    within = dot(later, dg_t, NN, EXACT)
    after_mat = (iota((width, width), 0) > iota((width, width), 1)).astype(F32)
    after = dot(jnp.broadcast_to(within[0:1, :], (8, width)), after_mat, NN, EXACT)
    dlogit = -(within + after[0:1, :]) / (1.0 + jnp.exp(-logit_t))

    total = zeros
    for b in range(heads):
        dcol = jnp.broadcast_to(dlogit[:, b : b + 1], (tok, width))
        total = total + dcol * rb[K, b].astype(F32)
        out_s[1, b] = (out_s[1, b].astype(F32) + dcol * gate).astype(BF16)

    dz = Along(z, at_z, dz_own, dz_slots, dz_s, dz_r)
    dy = Exchange(yn, yh, at_y, dy_own, dy_slots, dy_s, dy_r)
    dc = Exchange(heads, c, at_ctx, dc_own, dc_slots, dc_s, dc_r)
    dz.start(jnp.sum(total, axis=0, keepdims=True))

    def send_key(j, _):
        back(1, j, c, lax.rem(c + j, heads)).start()
        return 0

    lax.fori_loop(1, heads, send_key, 0)
    own_out(1).start()

    outs = (qo_out, ko_out)

    def join_heads(which):
        def go(j, _):
            s = lax.rem(c + j, heads)
            back(which, j, s, s).wait_recv()
            return 0

        lax.fori_loop(1, heads, go, 0)
        own_out(which).wait()
        for h in range(heads):
            raw32[pl.ds(h, tok, stride=heads), :] = out_r[which, h].astype(F32)
        packed[which] = raw32[...].astype(BF16)
        pltpu.make_async_copy(packed.at[which], outs[which], osem.at[which]).start()

    join_heads(0)
    dz.turn()
    dy.start(dz.finish())
    dy.finish()
    dc.start(jnp.sum(dy_slots[...], axis=0))
    join_heads(1)
    dc.finish()
    square[...] = jnp.zeros_like(square)
    square[0:heads, :] = dc_slots[...].reshape(heads, width)
    columns = square[...].T[:, 0:heads]
    at = iota((width, heads), 0)
    for e in range(2):
        gg_ref[e : e + 1, :] = jnp.sum(
            jnp.where(at == 2 * i + e, columns, 0.0), axis=0, keepdims=True
        )

    def drain(j, _):
        t = lax.rem(c + j, heads)
        for a in range(4):
            bulk(a, j, c, t).wait_send()
        for which in range(2):
            back(which, j, c, t).wait_send()
        return 0

    lax.fori_loop(1, heads, drain, 0)
    for which in range(2):
        pltpu.make_async_copy(packed.at[which], outs[which], osem.at[which]).wait()


def deliver(*refs):
    *pairs, sem = refs
    copies = [pltpu.make_async_copy(pairs[a], pairs[a + 3], sem.at[a]) for a in range(3)]
    for copy in copies:
        copy.start()
    for copy in copies:
        copy.wait()


def per_device(queries, keys, values, out_grad, gate_weight, head_bias):
    _, tok, heads, width = queries.shape
    yn = lax.axis_size("dp") // ZN
    rows = tok * heads
    flat = [x.reshape(rows, width) for x in (keys, values, out_grad, queries)]
    vm = pltpu.VMEM
    dma = pltpu.SemaphoreType.DMA

    def slots(n):
        return [vm((1, width), F32), vm((n, 1, width), F32)]

    along = [vm((3, 1, width), F32), vm((2 * REACH + 2, 1, width), F32)]
    ends = dma((2 * REACH + 2,))
    anywhere = pl.BlockSpec(memory_space=pl.ANY)
    far = pl.BlockSpec(memory_space=pltpu.HBM)
    inside = pl.BlockSpec(memory_space=pltpu.VMEM)
    held = [
        pltpu.with_memory_space_constraint(x, pltpu.HBM)
        for x in (*flat, gate_weight.T, head_bias.reshape(1, heads))
    ]
    qo, ko, gg = pl.pallas_call(
        kernel,
        name="history_grads",
        out_shape=(
            jax.ShapeDtypeStruct((rows, width), BF16),
            jax.ShapeDtypeStruct((rows, width), BF16),
            jax.ShapeDtypeStruct((2, heads), F32),
        ),
        in_specs=[far] * 6,
        out_specs=(anywhere, anywhere, inside),
        scratch_shapes=[
            vm((2, heads), BF16),
            vm((1, heads), BF16),
            vm((4, rows, width), BF16),
            vm((rows, width), F32),
            vm((4, heads, tok, width), BF16),
            vm((4, heads, tok, width), BF16),
            vm((heads, tok, width), F32),
            vm((heads, 1, width), F32),
            vm((heads, 1, width), F32),
            vm((heads, width, width), BF16),
            vm((heads, tok, tok), BF16),
            vm((heads, tok, width), F32),
            vm((heads, width, width), F32),
            vm((2, heads, tok, width), BF16),
            vm((2, heads, tok, width), BF16),
            vm((2, rows, width), BF16),
            vm((heads, width), F32),
            vm((width, width), F32),
            *slots(yn), *along, *along, *slots(yn), *slots(heads),
            dma((2,)), dma((4,)), dma((2,)),
            dma((4, heads)), dma((4, heads)),
            dma((2, heads)), dma((2, heads)),
            dma((4,)), dma((2,)),
            dma((yn,)), dma((yn,)), ends, ends,
            ends, ends, dma((yn,)), dma((yn,)), dma((heads,)), dma((heads,)),
        ],
        compiler_params=pltpu.CompilerParams(
            collective_id=0, has_side_effects=True, vmem_limit_bytes=48 * 1024 * 1024
        ),
    )(*held)
    outs = pl.pallas_call(
        deliver,
        name="deliver",
        out_shape=tuple(jax.ShapeDtypeStruct(x.shape, x.dtype) for x in (qo, ko, gg)),
        in_specs=[anywhere] * 3,
        out_specs=(far,) * 3,
        scratch_shapes=[dma((3,))],
        compiler_params=pltpu.CompilerParams(vmem_limit_bytes=1024 * 1024),
    )(qo, ko, gg)
    shape = (1, tok, heads, width)
    return outs[0].reshape(shape), outs[1].reshape(shape), outs[2].T


def solution(mesh):
    return jax.shard_map(
        per_device,
        mesh=mesh,
        in_specs=(
            P("dp", "ctx", None, None),
            P("dp", "ctx", None, None),
            P("dp", "ctx", None, None),
            P("dp", "ctx", None, None),
            P(None, "dp"),
            P(),
        ),
        out_specs=(P("dp", "ctx", None, None), P("dp", "ctx", None, None), P(None, "dp")),
        check_vma=False,
    )
```

```python
import functools

import jax
import jax.numpy as jnp
from jax import lax
from jax.experimental import pallas as pl
from jax.experimental.pallas import tpu as pltpu
from jax.sharding import PartitionSpec as P

F32 = jnp.float32
BF16 = jnp.bfloat16
MESH = pl.DeviceIdType.MESH
K, V, G, Q = 0, 1, 2, 3
ZN = 16
REACH = ZN // 4


def iota(shape, dim):
    return lax.broadcasted_iota(jnp.int32, shape, dim)


def dot(a, b, dims, precision=None):
    return lax.dot_general(
        a, b, (dims, ((), ())), precision=precision, preferred_element_type=F32
    )


NN = ((1,), (0,))
NT = ((1,), (1,))
TN = ((0,), (0,))
EXACT = lax.Precision.HIGHEST


def log1p(y):
    u = 1.0 + y
    d = u - 1.0
    return jnp.where(d == 0.0, y, jnp.log(u) * (y / jnp.where(d == 0.0, 1.0, d)))


class Along:
    def __init__(self, me, where, own, slots, ssem, rsem):
        self.me, self.where = me, where
        self.own, self.slots, self.ssem, self.rsem = own, slots, ssem, rsem

    def copy(self, src, j, step):
        return pltpu.make_async_remote_copy(
            src_ref=self.own.at[src],
            dst_ref=self.slots.at[j],
            send_sem=self.ssem.at[j],
            recv_sem=self.rsem.at[j],
            device_id=self.where(lax.rem(self.me + step + ZN, ZN)),
            device_id_type=MESH,
        )

    def near(self, j):
        return self.copy(0, j, jnp.where(j < REACH, j + 1, REACH - 1 - j))

    def start(self, row):
        self.own[0] = row

        def go(j, _):
            self.near(j).start()
            return 0

        lax.fori_loop(0, 2 * REACH, go, 0)

    def turn(self):
        def go(j, _):
            self.near(j).wait()
            return 0

        lax.fori_loop(0, 2 * REACH, go, 0)
        below = jnp.sum(self.slots[0:REACH], axis=0)
        above = jnp.sum(self.slots[REACH : 2 * REACH - 1], axis=0)
        self.own[1] = below
        self.own[2] = above
        self.far = [self.copy(1, 2 * REACH, REACH), self.copy(2, 2 * REACH + 1, -REACH)]
        for far in self.far:
            far.start()

    def finish(self):
        for far in self.far:
            far.wait()
        return self.own[0] + jnp.sum(self.slots[...], axis=0)


class Exchange:
    def __init__(self, n, me, where, own, slots, ssem, rsem):
        self.n, self.me, self.where = n, me, where
        self.own, self.slots, self.ssem, self.rsem = own, slots, ssem, rsem

    def start(self, row):
        self.own[...] = row
        self.slots[self.me] = row

        def go(j, _):
            pltpu.make_async_remote_copy(
                src_ref=self.own,
                dst_ref=self.slots.at[self.me],
                send_sem=self.ssem,
                recv_sem=self.rsem,
                device_id=self.where(lax.rem(self.me + j, self.n)),
                device_id_type=MESH,
            ).start()
            return 0

        lax.fori_loop(1, self.n, go, 0, unroll=3)

    def wait(self, sem):
        rows = self.slots.at[pl.ds(0, self.n - 1)]
        pltpu.make_async_copy(rows, rows, sem).wait()

    def finish(self):
        self.wait(self.rsem)

    def drain(self):
        self.wait(self.ssem)


def kernel(
    k_in, v_in, g_in, q_in, gw_in, hb_in,
    qo_out, ko_out, gg_ref,
    gw_v, hb_v, raw, raw32, sb, rb, colb, rowb, lastb, kvr, wts, qf, qgt, out_s, out_r, packed, lrow, square,
    wy_own, wy_slots, wz_own, wz_slots, dz_own, dz_slots, dc_own, dc_slots,
    ssem, lsem, osem, in_s, in_rs, back_s, back_rs, own_sem, own_back,
    wy_s, wy_r, wz_s, wz_r, dz_s, dz_r, dc_s, dc_r,
):
    yn = wy_slots.shape[0]
    heads = sb.shape[1]
    tok = sb.shape[2]
    width = sb.shape[3]
    scale = 1.0 / width
    i = lax.axis_index("dp")
    c = lax.axis_index("ctx")
    yh = i // ZN
    z = lax.rem(i, ZN)

    def at_ctx(t):
        return {"ctx": t}

    def at_z(t):
        return {"dp": yh * ZN + t}

    def at_y(t):
        return {"dp": t * ZN + z}

    loads = [
        pltpu.make_async_copy(src, raw.at[a], lsem.at[a])
        for a, src in enumerate((k_in, v_in, g_in, q_in))
    ]
    small = [
        pltpu.make_async_copy(src, dst, ssem.at[a])
        for a, (src, dst) in enumerate(((gw_in, gw_v), (hb_in, hb_v)))
    ]
    for load in small + loads:
        load.start()

    barrier = pltpu.get_barrier_semaphore()

    def greet_z(j, _):
        step = jnp.where(j < REACH, j + 1, REACH - 1 - j)
        pl.semaphore_signal(
            barrier, inc=1, device_id=at_z(lax.rem(z + step + ZN, ZN)), device_id_type=MESH
        )
        return 0

    lax.fori_loop(0, 2 * REACH, greet_z, 0)
    for n, me, where in ((yn, yh, at_y), (heads, c, at_ctx)):

        def greet(j, _, n=n, me=me, where=where):
            pl.semaphore_signal(
                barrier, inc=1, device_id=where(lax.rem(me + j, n)), device_id_type=MESH
            )
            return 0

        lax.fori_loop(1, n, greet, 0)

    for load in small:
        load.wait()
    gw = gw_v[...].astype(F32)
    picked = jnp.sum(jnp.where(iota(gw.shape, 1) == c, gw, 0.0), axis=1, keepdims=True)
    lane = iota((1, width), 1)
    own_row = jnp.where(lane == 2 * i, picked[0:1], 0.0) + jnp.where(
        lane == 2 * i + 1, picked[1:2], 0.0
    )
    hb = hb_v[...].astype(F32)
    bias = jnp.sum(jnp.where(iota(hb.shape, 1) == c, hb, 0.0), axis=1, keepdims=True)

    def split_heads(a):
        loads[a].wait()
        raw32[...] = raw[a].astype(F32)
        for h in range(heads):
            sb[a, h] = raw32[pl.ds(h, tok, stride=heads), :].astype(BF16)

    def bulk(a, j, slot, target):
        return pltpu.make_async_remote_copy(
            src_ref=sb.at[a, target],
            dst_ref=rb.at[a, slot],
            send_sem=in_s.at[a, j],
            recv_sem=in_rs.at[a, slot],
            device_id=at_ctx(target),
            device_id_type=MESH,
        )

    def own_in(a):
        return pltpu.make_async_copy(sb.at[a, c], rb.at[a, c], own_sem.at[a])

    def send_heads(a):
        def go(j, _):
            bulk(a, j, c, lax.rem(c + j, heads)).start()
            return 0

        lax.fori_loop(1, heads, go, 0)
        own_in(a).start()

    def wait_heads(a):
        def go(j, _):
            s = lax.rem(c + j, heads)
            bulk(a, j, s, s).wait_recv()
            return 0

        lax.fori_loop(1, heads, go, 0)
        own_in(a).wait()

    wy = Exchange(yn, yh, at_y, wy_own, wy_slots, wy_s, wy_r)
    wz = Along(z, at_z, wz_own, wz_slots, wz_s, wz_r)
    split_heads(K)
    pl.semaphore_wait(barrier, 2 * REACH + (yn - 1) + (heads - 1))
    wy.start(own_row)
    send_heads(K)
    split_heads(V)
    send_heads(V)
    wy.finish()
    wz.start(jnp.sum(wy_slots[...], axis=0))
    split_heads(G)
    send_heads(G)
    split_heads(Q)
    send_heads(Q)
    wz.turn()
    gate = wz.finish()

    wait_heads(K)
    gate8 = jnp.broadcast_to(gate, (8, width)).astype(BF16)
    for b in range(heads):
        lrow[b : b + 1, :] = dot(gate8, rb[K, b], NT)[0:1]
    logit = lrow[...] + bias
    decay = -(jnp.maximum(logit, 0.0) + log1p(jnp.exp(-jnp.abs(logit))))
    upper = (iota((tok, tok), 0) <= iota((tok, tok), 1)).astype(F32)
    cumul = dot(decay, upper, NN, EXACT)
    square[...] = jnp.zeros_like(square)
    square[0:heads, :] = cumul
    cumul_t = square[...].T
    square[0:heads, :] = logit
    logit_t = square[...].T
    for b in range(heads):
        colb[b] = jnp.broadcast_to(cumul_t[:, b : b + 1], (tok, width))
        rowb[b] = cumul[b : b + 1, :]
        lastb[b] = jnp.broadcast_to(cumul[b : b + 1, tok - 1 : tok], (1, width))

    wait_heads(V)

    def forward(b, state):
        kvr[b] = state.astype(BF16)
        tail = jnp.exp(lastb[b] - colb[b])
        scaled = (rb[K, b].astype(F32) * tail).astype(BF16)
        return jnp.exp(lastb[b]) * state + dot(rb[V, b], scaled, TN)

    lax.fori_loop(0, heads, forward, jnp.zeros((width, width), F32), unroll=4)

    wait_heads(G)

    def back(which, j, slot, target):
        return pltpu.make_async_remote_copy(
            src_ref=out_s.at[which, target],
            dst_ref=out_r.at[which, slot],
            send_sem=back_s.at[which, j],
            recv_sem=back_rs.at[which, slot],
            device_id=at_ctx(target),
            device_id_type=MESH,
        )

    def own_out(which):
        return pltpu.make_async_copy(out_s.at[which, c], out_r.at[which, c], own_back.at[which])

    causal = iota((tok, tok), 0) >= iota((tok, tok), 1)

    def query_block(b):
        kx, vx, gx = rb[K, b], rb[V, b], rb[G, b]
        gap = colb[b] - rowb[b]
        fade = jnp.exp(jnp.where(causal, gap, -1e30))
        weight = (scale * dot(gx, vx, NT) * fade).astype(BF16)
        wts[b] = weight
        full = dot(weight, kx, NN) + scale * jnp.exp(colb[b]) * dot(gx, kvr[b], NN)
        qf[b] = full
        out_s[0, b] = full.astype(BF16)

    def query_step(j, _):
        query_block(j)
        return 0

    lax.fori_loop(0, heads, query_step, 0, unroll=4)

    zeros = jnp.zeros((width, width), F32)

    def arrival(b, dg_t):
        gx, qx = rb[G, b], rb[Q, b]
        qx32 = qx.astype(F32)
        diff = jnp.sum(qx32 * qf[b], axis=1, keepdims=True)
        qf[b] = dot(wts[b], qx, TN)
        qgt[b] = dot(gx, (qx32 * jnp.exp(colb[b])).astype(BF16), TN)
        return jnp.where(iota(dg_t.shape, 1) == b, diff, dg_t)

    own_in(Q).wait()

    def arrival_step(j, dg_t):
        s = lax.rem(c + heads - j, heads)
        bulk(Q, j, s, s).wait_recv()
        return arrival(s, dg_t)

    dg_t = lax.fori_loop(1, heads, arrival_step, arrival(c, zeros), unroll=3)

    def send_back(which):
        def go(j, _):
            back(which, j, c, lax.rem(c + j, heads)).start()
            return 0

        lax.fori_loop(1, heads, go, 0)
        own_out(which).start()

    send_back(0)

    def backward(j, carry):
        b = heads - 1 - j
        state, dg_t = carry
        last = lastb[b]
        tail = jnp.exp(last - colb[b])
        kattn = qf[b] + scale * tail * dot(rb[V, b], state.astype(BF16), NN)
        out_s[1, b] = kattn.astype(BF16)
        diff = jnp.sum(rb[K, b].astype(F32) * kattn, axis=1, keepdims=True)
        dg_t = dg_t - jnp.where(iota(dg_t.shape, 1) == b, diff, 0.0)
        return jnp.exp(last) * state + qgt[b], dg_t

    _, dg_t = lax.fori_loop(0, heads, backward, (zeros, dg_t), unroll=4)

    later = (iota((tok, tok), 0) <= iota((tok, tok), 1)).astype(F32)
    within = dot(later, dg_t, NN, EXACT)
    after_mat = (iota((width, width), 0) > iota((width, width), 1)).astype(F32)
    after = dot(jnp.broadcast_to(within[0:1, :], (8, width)), after_mat, NN, EXACT)
    dlogit = -(within + after[0:1, :]) / (1.0 + jnp.exp(-logit_t))

    total = zeros
    for b in range(heads):
        dcol = jnp.broadcast_to(dlogit[:, b : b + 1], (tok, width))
        total = total + dcol * rb[K, b].astype(F32)
        out_s[1, b] = (out_s[1, b].astype(F32) + dcol * gate).astype(BF16)

    dz = Exchange(ZN, z, at_z, dz_own, dz_slots, dz_s, dz_r)
    def at_cell(t):
        return {"dp": t // heads * ZN + z, "ctx": lax.rem(t, heads)}

    dc = Exchange(yn * heads, yh * heads + c, at_cell, dc_own, dc_slots, dc_s, dc_r)
    dz.start(jnp.sum(total, axis=0, keepdims=True))

    send_back(1)
    outs = (qo_out, ko_out)

    def join_heads(which):
        def go(j, _):
            s = lax.rem(c + j, heads)
            back(which, j, s, s).wait_recv()
            return 0

        lax.fori_loop(1, heads, go, 0)
        own_out(which).wait()
        for h in range(heads):
            raw32[pl.ds(h, tok, stride=heads), :] = out_r[which, h].astype(F32)
        packed[which] = raw32[...].astype(BF16)
        pltpu.make_async_copy(packed.at[which], outs[which], osem.at[which]).start()

    join_heads(0)
    dz.finish()
    dc.start(jnp.sum(dz_slots[...], axis=0))
    join_heads(1)
    dc.finish()
    rows = jnp.sum(dc_slots[...].reshape(yn, heads, width), axis=0)
    square[...] = jnp.zeros_like(square)
    square[0:heads, :] = rows
    columns = square[...].T[:, 0:heads]
    at = iota((width, heads), 0)
    for e in range(2):
        gg_ref[e : e + 1, :] = jnp.sum(
            jnp.where(at == 2 * i + e, columns, 0.0), axis=0, keepdims=True
        )

    for small_exchange in (wy, dz, dc):
        small_exchange.drain()

    def drain(j, _):
        t = lax.rem(c + j, heads)
        for a in range(4):
            bulk(a, j, c, t).wait_send()
        for which in range(2):
            back(which, j, c, t).wait_send()
        return 0

    lax.fori_loop(1, heads, drain, 0)
    for which in range(2):
        pltpu.make_async_copy(packed.at[which], outs[which], osem.at[which]).wait()


def deliver(*refs):
    *pairs, sem = refs
    copies = [pltpu.make_async_copy(pairs[a], pairs[a + 3], sem.at[a]) for a in range(3)]
    for copy in copies:
        copy.start()
    for copy in copies:
        copy.wait()


def per_device(queries, keys, values, out_grad, gate_weight, head_bias):
    _, tok, heads, width = queries.shape
    yn = lax.axis_size("dp") // ZN
    rows = tok * heads
    flat = [x.reshape(rows, width) for x in (keys, values, out_grad, queries)]
    vm = pltpu.VMEM
    dma = pltpu.SemaphoreType.DMA

    def slots(n):
        return [vm((1, width), F32), vm((n, 1, width), F32)]

    along = [vm((3, 1, width), F32), vm((2 * REACH + 2, 1, width), F32)]
    ends = dma((2 * REACH + 2,))
    one = dma(())
    anywhere = pl.BlockSpec(memory_space=pl.ANY)
    far = pl.BlockSpec(memory_space=pltpu.HBM)
    inside = pl.BlockSpec(memory_space=pltpu.VMEM)
    held = [
        pltpu.with_memory_space_constraint(x, pltpu.HBM)
        for x in (*flat, gate_weight.T, head_bias.reshape(1, heads))
    ]
    qo, ko, gg = pl.pallas_call(
        kernel,
        name="history_grads",
        out_shape=(
            jax.ShapeDtypeStruct((rows, width), BF16),
            jax.ShapeDtypeStruct((rows, width), BF16),
            jax.ShapeDtypeStruct((2, heads), F32),
        ),
        in_specs=[far] * 6,
        out_specs=(anywhere, anywhere, inside),
        scratch_shapes=[
            vm((2, heads), BF16),
            vm((1, heads), BF16),
            vm((4, rows, width), BF16),
            vm((rows, width), F32),
            vm((4, heads, tok, width), BF16),
            vm((4, heads, tok, width), BF16),
            vm((heads, tok, width), F32),
            vm((heads, 1, width), F32),
            vm((heads, 1, width), F32),
            vm((heads, width, width), BF16),
            vm((heads, tok, tok), BF16),
            vm((heads, tok, width), F32),
            vm((heads, width, width), F32),
            vm((2, heads, tok, width), BF16),
            vm((2, heads, tok, width), BF16),
            vm((2, rows, width), BF16),
            vm((heads, width), F32),
            vm((width, width), F32),
            *slots(yn), *along, *slots(ZN), *slots(yn * heads),
            dma((2,)), dma((4,)), dma((2,)),
            dma((4, heads)), dma((4, heads)),
            dma((2, heads)), dma((2, heads)),
            dma((4,)), dma((2,)),
            one, one, ends, ends, one, one, one, one,
        ],
        compiler_params=pltpu.CompilerParams(
            collective_id=0, has_side_effects=True, vmem_limit_bytes=48 * 1024 * 1024
        ),
    )(*held)
    outs = pl.pallas_call(
        deliver,
        name="deliver",
        out_shape=tuple(jax.ShapeDtypeStruct(x.shape, x.dtype) for x in (qo, ko, gg)),
        in_specs=[anywhere] * 3,
        out_specs=(far,) * 3,
        scratch_shapes=[dma((3,))],
        compiler_params=pltpu.CompilerParams(vmem_limit_bytes=1024 * 1024),
    )(qo, ko, gg)
    shape = (1, tok, heads, width)
    return outs[0].reshape(shape), outs[1].reshape(shape), outs[2].T


def solution(mesh):
    return jax.shard_map(
        per_device,
        mesh=mesh,
        in_specs=(
            P("dp", "ctx", None, None),
            P("dp", "ctx", None, None),
            P("dp", "ctx", None, None),
            P("dp", "ctx", None, None),
            P(None, "dp"),
            P(),
        ),
        out_specs=(P("dp", "ctx", None, None), P("dp", "ctx", None, None), P(None, "dp")),
        check_vma=False,
    )
```

```python
import functools

import jax
import jax.numpy as jnp
from jax import lax
from jax.experimental import pallas as pl
from jax.experimental.pallas import tpu as pltpu
from jax.sharding import PartitionSpec as P

F32 = jnp.float32
BF16 = jnp.bfloat16
MESH = pl.DeviceIdType.MESH
K, V, G, Q = 0, 1, 2, 3
PIECES = 4
ZN = 16
REACH = ZN // 4


def iota(shape, dim):
    return lax.broadcasted_iota(jnp.int32, shape, dim)


def dot(a, b, dims, precision=None):
    return lax.dot_general(
        a, b, (dims, ((), ())), precision=precision, preferred_element_type=F32
    )


NN = ((1,), (0,))
NT = ((1,), (1,))
TN = ((0,), (0,))
EXACT = lax.Precision.HIGHEST


def log1p(y):
    u = 1.0 + y
    d = u - 1.0
    return jnp.where(d == 0.0, y, jnp.log(u) * (y / jnp.where(d == 0.0, 1.0, d)))


class Along:
    def __init__(self, me, where, own, slots, ssem, rsem):
        self.me, self.where = me, where
        self.own, self.slots, self.ssem, self.rsem = own, slots, ssem, rsem

    def copy(self, src, j, step):
        return pltpu.make_async_remote_copy(
            src_ref=self.own.at[src],
            dst_ref=self.slots.at[j],
            send_sem=self.ssem.at[j],
            recv_sem=self.rsem.at[j],
            device_id=self.where(lax.rem(self.me + step + ZN, ZN)),
            device_id_type=MESH,
        )

    def near(self, j):
        return self.copy(0, j, jnp.where(j < REACH, j + 1, REACH - 1 - j))

    def start(self, row):
        self.own[0] = row

        def go(j, _):
            self.near(j).start()
            return 0

        lax.fori_loop(0, 2 * REACH, go, 0)

    def turn(self):
        def go(j, _):
            self.near(j).wait()
            return 0

        lax.fori_loop(0, 2 * REACH, go, 0)
        below = jnp.sum(self.slots[0:REACH], axis=0)
        above = jnp.sum(self.slots[REACH : 2 * REACH - 1], axis=0)
        self.own[1] = below
        self.own[2] = above
        self.far = [self.copy(1, 2 * REACH, REACH), self.copy(2, 2 * REACH + 1, -REACH)]
        for far in self.far:
            far.start()

    def finish(self):
        for far in self.far:
            far.wait()
        return self.own[0] + jnp.sum(self.slots[...], axis=0)


class Exchange:
    def __init__(self, n, me, where, own, slots, ssem, rsem):
        self.n, self.me, self.where = n, me, where
        self.own, self.slots, self.ssem, self.rsem = own, slots, ssem, rsem

    def start(self, row):
        self.own[...] = row
        self.slots[self.me] = row

        def go(j, _):
            pltpu.make_async_remote_copy(
                src_ref=self.own,
                dst_ref=self.slots.at[self.me],
                send_sem=self.ssem,
                recv_sem=self.rsem,
                device_id=self.where(lax.rem(self.me + j, self.n)),
                device_id_type=MESH,
            ).start()
            return 0

        lax.fori_loop(1, self.n, go, 0, unroll=3)

    def wait(self, sem):
        rows = self.slots.at[pl.ds(0, self.n - 1)]
        pltpu.make_async_copy(rows, rows, sem).wait()

    def finish(self):
        self.wait(self.rsem)

    def drain(self):
        self.wait(self.ssem)


def kernel(
    k_in, v_in, g_in, q_in, gw_in, hb_in,
    qo_out, ko_out, gg_ref,
    gw_v, hb_v, raw, raw32, sb, rb, colb, rowb, lastb, kvr, wts, qf, qgt, out_s, out_r, packed, lrow, square,
    wy_own, wy_slots, wz_own, wz_slots, dz_own, dz_slots, dc_own, dc_slots,
    ssem, lsem, osem, in_s, in_rs, back_s, back_rs, own_sem, own_back,
    wy_s, wy_r, wz_s, wz_r, dz_s, dz_r, dc_s, dc_r,
):
    yn = wy_slots.shape[0]
    heads = sb.shape[1]
    tok = sb.shape[2]
    width = sb.shape[3]
    scale = 1.0 / width
    i = lax.axis_index("dp")
    c = lax.axis_index("ctx")
    yh = i // ZN
    z = lax.rem(i, ZN)

    def at_ctx(t):
        return {"ctx": t}

    def at_z(t):
        return {"dp": yh * ZN + t}

    def at_y(t):
        return {"dp": t * ZN + z}

    loads = [
        pltpu.make_async_copy(src, raw.at[a], lsem.at[a])
        for a, src in enumerate((k_in, v_in, g_in, q_in))
    ]
    small = [
        pltpu.make_async_copy(src, dst, ssem.at[a])
        for a, (src, dst) in enumerate(((gw_in, gw_v), (hb_in, hb_v)))
    ]
    for load in small + loads:
        load.start()

    barrier = pltpu.get_barrier_semaphore()

    def greet_z(j, _):
        step = jnp.where(j < REACH, j + 1, REACH - 1 - j)
        pl.semaphore_signal(
            barrier, inc=1, device_id=at_z(lax.rem(z + step + ZN, ZN)), device_id_type=MESH
        )
        return 0

    lax.fori_loop(0, 2 * REACH, greet_z, 0)
    for n, me, where in ((yn, yh, at_y), (heads, c, at_ctx)):

        def greet(j, _, n=n, me=me, where=where):
            pl.semaphore_signal(
                barrier, inc=1, device_id=where(lax.rem(me + j, n)), device_id_type=MESH
            )
            return 0

        lax.fori_loop(1, n, greet, 0)

    for load in small:
        load.wait()
    gw = gw_v[...].astype(F32)
    picked = jnp.sum(jnp.where(iota(gw.shape, 1) == c, gw, 0.0), axis=1, keepdims=True)
    lane = iota((1, width), 1)
    own_row = jnp.where(lane == 2 * i, picked[0:1], 0.0) + jnp.where(
        lane == 2 * i + 1, picked[1:2], 0.0
    )
    hb = hb_v[...].astype(F32)
    bias = jnp.sum(jnp.where(iota(hb.shape, 1) == c, hb, 0.0), axis=1, keepdims=True)

    def split_heads(a):
        loads[a].wait()
        raw32[...] = raw[a].astype(F32)
        for h in range(heads):
            sb[a, h] = raw32[pl.ds(h, tok, stride=heads), :].astype(BF16)

    def bulk(a, j, slot, target):
        return pltpu.make_async_remote_copy(
            src_ref=sb.at[a, target],
            dst_ref=rb.at[a, slot],
            send_sem=in_s.at[a, j],
            recv_sem=in_rs.at[a, slot],
            device_id=at_ctx(target),
            device_id_type=MESH,
        )

    def own_in(a):
        return pltpu.make_async_copy(sb.at[a, c], rb.at[a, c], own_sem.at[a])

    def send_heads(a):
        def go(j, _):
            bulk(a, j, c, lax.rem(c + j, heads)).start()
            return 0

        lax.fori_loop(1, heads, go, 0)
        own_in(a).start()

    def wait_heads(a):
        def go(j, _):
            s = lax.rem(c + j, heads)
            bulk(a, j, s, s).wait_recv()
            return 0

        lax.fori_loop(1, heads, go, 0)
        own_in(a).wait()

    wy = Exchange(yn, yh, at_y, wy_own, wy_slots, wy_s, wy_r)
    wz = Along(z, at_z, wz_own, wz_slots, wz_s, wz_r)
    split_heads(K)
    pl.semaphore_wait(barrier, 2 * REACH + (yn - 1) + (heads - 1))
    wy.start(own_row)
    send_heads(K)
    split_heads(V)
    split_heads(G)
    split_heads(Q)
    wy.finish()
    wz.start(jnp.sum(wy_slots[...], axis=0))
    send_heads(V)
    wz.turn()
    send_heads(G)
    send_heads(Q)
    gate = wz.finish()

    wait_heads(K)
    gate8 = jnp.broadcast_to(gate, (8, width)).astype(BF16)
    for b in range(heads):
        lrow[b : b + 1, :] = dot(gate8, rb[K, b], NT)[0:1]
    logit = lrow[...] + bias
    decay = -(jnp.maximum(logit, 0.0) + log1p(jnp.exp(-jnp.abs(logit))))
    upper = (iota((tok, tok), 0) <= iota((tok, tok), 1)).astype(F32)
    cumul = dot(decay, upper, NN, EXACT)
    square[...] = jnp.zeros_like(square)
    square[0:heads, :] = cumul
    cumul_t = square[...].T
    square[0:heads, :] = logit
    logit_t = square[...].T
    for b in range(heads):
        colb[b] = jnp.broadcast_to(cumul_t[:, b : b + 1], (tok, width))
        rowb[b] = cumul[b : b + 1, :]
        lastb[b] = jnp.broadcast_to(cumul[b : b + 1, tok - 1 : tok], (1, width))

    wait_heads(V)

    def forward(b, state):
        kvr[b] = state.astype(BF16)
        tail = jnp.exp(lastb[b] - colb[b])
        scaled = (rb[K, b].astype(F32) * tail).astype(BF16)
        return jnp.exp(lastb[b]) * state + dot(rb[V, b], scaled, TN)

    lax.fori_loop(0, heads, forward, jnp.zeros((width, width), F32), unroll=4)

    wait_heads(G)

    def back(which, j, slot, target):
        return pltpu.make_async_remote_copy(
            src_ref=out_s.at[which, target],
            dst_ref=out_r.at[which, slot],
            send_sem=back_s.at[which, j],
            recv_sem=back_rs.at[which, slot],
            device_id=at_ctx(target),
            device_id_type=MESH,
        )

    def own_out(which):
        return pltpu.make_async_copy(out_s.at[which, c], out_r.at[which, c], own_back.at[which])

    causal = iota((tok, tok), 0) >= iota((tok, tok), 1)

    def query_block(b):
        kx, vx, gx = rb[K, b], rb[V, b], rb[G, b]
        gap = colb[b] - rowb[b]
        fade = jnp.exp(jnp.where(causal, gap, -1e30))
        weight = (scale * dot(gx, vx, NT) * fade).astype(BF16)
        wts[b] = weight
        full = dot(weight, kx, NN) + scale * jnp.exp(colb[b]) * dot(gx, kvr[b], NN)
        qf[b] = full
        out_s[0, b] = full.astype(BF16)

    def query_step(j, _):
        query_block(j)
        return 0

    lax.fori_loop(0, heads, query_step, 0, unroll=4)

    def send_back(which):
        def go(j, _):
            back(which, j, c, lax.rem(c + j, heads)).start()
            return 0

        lax.fori_loop(1, heads, go, 0)
        own_out(which).start()

    send_back(0)

    zeros = jnp.zeros((width, width), F32)

    def arrival(b, dg_t):
        gx, qx = rb[G, b], rb[Q, b]
        qx32 = qx.astype(F32)
        diff = jnp.sum(qx32 * qf[b], axis=1, keepdims=True)
        qf[b] = dot(wts[b], qx, TN)
        qgt[b] = dot(gx, (qx32 * jnp.exp(colb[b])).astype(BF16), TN)
        return jnp.where(iota(dg_t.shape, 1) == b, diff, dg_t)

    own_in(Q).wait()

    def arrival_step(j, dg_t):
        s = lax.rem(c + heads - j, heads)
        bulk(Q, j, s, s).wait_recv()
        return arrival(s, dg_t)

    dg_t = lax.fori_loop(1, heads, arrival_step, arrival(c, zeros), unroll=3)

    def backward(j, carry):
        b = heads - 1 - j
        state, dg_t = carry
        last = lastb[b]
        tail = jnp.exp(last - colb[b])
        kattn = qf[b] + scale * tail * dot(rb[V, b], state.astype(BF16), NN)
        out_s[1, b] = kattn.astype(BF16)
        diff = jnp.sum(rb[K, b].astype(F32) * kattn, axis=1, keepdims=True)
        dg_t = dg_t - jnp.where(iota(dg_t.shape, 1) == b, diff, 0.0)
        return jnp.exp(last) * state + qgt[b], dg_t

    _, dg_t = lax.fori_loop(0, heads, backward, (zeros, dg_t), unroll=4)

    later = (iota((tok, tok), 0) <= iota((tok, tok), 1)).astype(F32)
    within = dot(later, dg_t, NN, EXACT)
    after_mat = (iota((width, width), 0) > iota((width, width), 1)).astype(F32)
    after = dot(jnp.broadcast_to(within[0:1, :], (8, width)), after_mat, NN, EXACT)
    dlogit = -(within + after[0:1, :]) / (1.0 + jnp.exp(-logit_t))

    total = zeros
    for b in range(heads):
        dcol = jnp.broadcast_to(dlogit[:, b : b + 1], (tok, width))
        total = total + dcol * rb[K, b].astype(F32)

    dz = Exchange(ZN, z, at_z, dz_own, dz_slots, dz_s, dz_r)
    dz.start(jnp.sum(total, axis=0, keepdims=True))

    for b in range(heads):
        dcol = jnp.broadcast_to(dlogit[:, b : b + 1], (tok, width))
        out_s[1, b] = (out_s[1, b].astype(F32) + dcol * gate).astype(BF16)
    send_back(1)
    outs = (qo_out, ko_out)

    def join_heads(which):
        def go(j, _):
            s = lax.rem(c + j, heads)
            back(which, j, s, s).wait_recv()
            return 0

        lax.fori_loop(1, heads, go, 0)
        own_out(which).wait()
        for h in range(heads):
            raw32[pl.ds(h, tok, stride=heads), :] = out_r[which, h].astype(F32)
        packed[which] = raw32[...].astype(BF16)
        pltpu.make_async_copy(packed.at[which], outs[which], osem.at[which]).start()

    join_heads(0)
    dz.finish()
    row = jnp.sum(dz_slots[...], axis=0)
    dc_own[...] = row
    mine = yh * heads + c
    dc_slots[mine] = row

    def to_cell(y, t):
        pltpu.make_async_remote_copy(
            src_ref=dc_own,
            dst_ref=dc_slots.at[mine],
            send_sem=dc_s,
            recv_sem=dc_r,
            device_id={"dp": y * ZN + z, "ctx": t},
            device_id_type=MESH,
        ).start()
        return 0

    for step in (2, 1, 3):
        y = lax.rem(yh + step, yn)
        lax.fori_loop(0, heads, lambda t, _, y=y: to_cell(y, t), 0, unroll=8)
    lax.fori_loop(1, heads, lambda j, _: to_cell(yh, lax.rem(c + j, heads)), 0, unroll=5)

    def wait_cells(sem):
        others = dc_slots.at[pl.ds(0, yn * heads - 1)]
        pltpu.make_async_copy(others, others, sem).wait()

    join_heads(1)
    for exchange in (wy, dz):
        exchange.drain()

    def drain(j, _):
        t = lax.rem(c + j, heads)
        for a in range(4):
            bulk(a, j, c, t).wait_send()
        for which in range(2):
            back(which, j, c, t).wait_send()
        return 0

    lax.fori_loop(1, heads, drain, 0)
    for which in range(2):
        pltpu.make_async_copy(packed.at[which], outs[which], osem.at[which]).wait()
    wait_cells(dc_r)
    rows = jnp.sum(dc_slots[...].reshape(yn, heads, width), axis=0)
    square[...] = jnp.zeros_like(square)
    square[0:heads, :] = rows
    columns = square[...].T[:, 0:heads]
    at = iota((width, heads), 0)
    for e in range(2):
        gg_ref[e : e + 1, :] = jnp.sum(
            jnp.where(at == 2 * i + e, columns, 0.0), axis=0, keepdims=True
        )

    wait_cells(dc_s)


def deliver(qo, ko, gg, qo_out, ko_out, gg_out, sem):
    rows = qo.shape[0] // PIECES
    copies = [pltpu.make_async_copy(gg, gg_out, sem.at[2 * PIECES])]
    for piece in range(PIECES):
        part = pl.ds(piece * rows, rows)
        for which, (src, dst) in enumerate(((qo, qo_out), (ko, ko_out))):
            at = sem.at[2 * piece + which]
            copies.append(pltpu.make_async_copy(src.at[part], dst.at[part], at))
    for copy in copies:
        copy.start()
    for copy in copies:
        copy.wait()


def per_device(queries, keys, values, out_grad, gate_weight, head_bias):
    _, tok, heads, width = queries.shape
    yn = lax.axis_size("dp") // ZN
    rows = tok * heads
    flat = [x.reshape(rows, width) for x in (keys, values, out_grad, queries)]
    vm = pltpu.VMEM
    dma = pltpu.SemaphoreType.DMA

    def slots(n):
        return [vm((1, width), F32), vm((n, 1, width), F32)]

    along = [vm((3, 1, width), F32), vm((2 * REACH + 2, 1, width), F32)]
    ends = dma((2 * REACH + 2,))
    one = dma(())
    anywhere = pl.BlockSpec(memory_space=pl.ANY)
    far = pl.BlockSpec(memory_space=pltpu.HBM)
    inside = pl.BlockSpec(memory_space=pltpu.VMEM)
    held = [
        pltpu.with_memory_space_constraint(x, pltpu.HBM)
        for x in (*flat, gate_weight.T, head_bias.reshape(1, heads))
    ]
    qo, ko, gg = pl.pallas_call(
        kernel,
        name="history_grads",
        out_shape=(
            jax.ShapeDtypeStruct((rows, width), BF16),
            jax.ShapeDtypeStruct((rows, width), BF16),
            jax.ShapeDtypeStruct((2, heads), F32),
        ),
        in_specs=[far] * 6,
        out_specs=(anywhere, anywhere, inside),
        scratch_shapes=[
            vm((2, heads), BF16),
            vm((1, heads), BF16),
            vm((4, rows, width), BF16),
            vm((rows, width), F32),
            vm((4, heads, tok, width), BF16),
            vm((4, heads, tok, width), BF16),
            vm((heads, tok, width), F32),
            vm((heads, 1, width), F32),
            vm((heads, 1, width), F32),
            vm((heads, width, width), BF16),
            vm((heads, tok, tok), BF16),
            vm((heads, tok, width), F32),
            vm((heads, width, width), F32),
            vm((2, heads, tok, width), BF16),
            vm((2, heads, tok, width), BF16),
            vm((2, rows, width), BF16),
            vm((heads, width), F32),
            vm((width, width), F32),
            *slots(yn), *along, *slots(ZN), *slots(yn * heads),
            dma((2,)), dma((4,)), dma((2,)),
            dma((4, heads)), dma((4, heads)),
            dma((2, heads)), dma((2, heads)),
            dma((4,)), dma((2,)),
            one, one, ends, ends, one, one, one, one,
        ],
        compiler_params=pltpu.CompilerParams(
            collective_id=0, has_side_effects=True, vmem_limit_bytes=48 * 1024 * 1024
        ),
    )(*held)
    outs = pl.pallas_call(
        deliver,
        name="deliver",
        out_shape=tuple(jax.ShapeDtypeStruct(x.shape, x.dtype) for x in (qo, ko, gg)),
        in_specs=[anywhere] * 3,
        out_specs=(far,) * 3,
        scratch_shapes=[dma((2 * PIECES + 1,))],
        compiler_params=pltpu.CompilerParams(vmem_limit_bytes=1024 * 1024),
    )(qo, ko, gg)
    shape = (1, tok, heads, width)
    return outs[0].reshape(shape), outs[1].reshape(shape), outs[2].T


def solution(mesh):
    return jax.shard_map(
        per_device,
        mesh=mesh,
        in_specs=(
            P("dp", "ctx", None, None),
            P("dp", "ctx", None, None),
            P("dp", "ctx", None, None),
            P("dp", "ctx", None, None),
            P(None, "dp"),
            P(),
        ),
        out_specs=(P("dp", "ctx", None, None), P("dp", "ctx", None, None), P(None, "dp")),
        check_vma=False,
    )
```
